256 devices in a mesh: row: 2 (over core), col: 8 (over z), cuts: 16 (over y, x).
Axes of the slice: x: 4, y: 4, z: 8, core: 2. Of those that a mesh axis runs over, the one named last changes fastest.
Arguments:
- y_blocks: bfloat16 [128, 12, 128, 128], P('cuts', None, ('row', 'col')), may hold values from -0.5 to 0.5
- z_blocks: bfloat16 [128, 12, 128, 128], P('cuts', None, ('row', 'col')), may hold values from -0.59765625 to 0.59765625
- pattern: int32 [128, 12], replicated, may hold values from 0 to 127, as said below
Outputs:
- z_next: bfloat16 [128, 12, 128, 128], P('cuts', None, ('row', 'col'))
The draws below stay inside these ranges and needn't reach their ends.
Inputs may be any that keep to these rules, and one draw needn't show every extreme that they name: `pattern`: row i lists 12 distinct block columns, i among them, each equal to i + d modulo 128 for some d with -6 <= d <= 6.
All inputs are finite; a program needn't handle non-finite values.
Results may differ from the reference program's by a relative error of at most 0.0049.
Values may be sent and summed in bfloat16 or wider, within the bound.
A program may use at most 64 MiB of HBM per device.

```python
import jax
import jax.numpy as jnp
from jax import lax

BLK = 128
KB = 12
HALO = 6
NB = 128


def draw_pattern(key, part):
    scores = jax.random.randint(key, (NB, 2 * HALO), 0, 1 << 20, dtype=jnp.int32)
    scores = scores * (2 * HALO) + jnp.arange(2 * HALO, dtype=jnp.int32)[None, :]
    picked = jax.lax.top_k(scores, KB - 1)[1].astype(jnp.int32)
    offsets = jnp.where(picked < HALO, picked - HALO, picked - HALO + 1).astype(jnp.int32)
    offsets = jnp.concatenate([jnp.zeros((NB, 1), jnp.int32), offsets], axis=1)
    row_numbers = jnp.arange(NB, dtype=jnp.int32)[:, None]
    return ((row_numbers + offsets) % NB).astype(jnp.int32)


def steps_of(key, shape, split, least, top_value):
    factor_of, own = 1.0, jax.random.fold_in(key, 6)
    for axis_at, parts in split:
        draws = jnp.exp(jax.random.uniform(jax.random.fold_in(own, axis_at), (parts,), jnp.float32, least / len(split), top_value / len(split)))
        factor_of = factor_of * jnp.repeat(draws, shape[axis_at] // parts).reshape([-1 if axis == axis_at else 1 for axis in range(len(shape))])
    return factor_of


def noise(own_key, extent, scale, reach, split=(), held_as=jnp.bfloat16):
    values = scale * jax.random.normal(own_key, extent, jnp.float32)
    if split:
        values = values * steps_of(own_key, extent, split, -0.22, 0.18)
    return jnp.clip(values, -reach, reach).astype(held_as)


def setup_inputs(seed: int = 0) -> dict:
    seeds = jax.random.split(jax.random.key(seed), 4)
    return {
        "y_blocks": noise(seeds[0], (NB, KB, BLK, BLK), BLK ** -0.5, 0.5, ((0, 16), (2, 16))),
        "z_blocks": noise(seeds[1], (NB, KB, BLK, BLK), 0.1, 0.59765625, ((0, 16), (2, 16))),
        "pattern": draw_pattern(jax.random.fold_in(seeds[3], 71), 0),
    }


def pattern_product(left_blocks, right_blocks, pattern):
    def one_row(row_number):
        listed = pattern[row_number]
        left_rows = left_blocks[row_number].astype(jnp.float32)
        right_rows = right_blocks[listed].astype(jnp.float32)
        right_cols = pattern[listed]
        matching = (right_cols[:, :, None] == listed[None, None, :]).astype(jnp.float32)
        selected = jnp.einsum('mnq,mnbe->mqbe', matching, right_rows, precision=lax.Precision.HIGHEST)
        return jnp.einsum('mab,mqbe->qae', left_rows, selected, precision=lax.Precision.HIGHEST)
    return lax.map(one_row, jnp.arange(NB, dtype=jnp.int32))


def reference(y_blocks, z_blocks, pattern):
    product = pattern_product(y_blocks, z_blocks, pattern)
    row_numbers = jnp.arange(NB, dtype=jnp.int32)
    diagonal = (pattern == row_numbers[:, None]).astype(jnp.float32)
    inside = jnp.arange(BLK, dtype=jnp.int32)
    eye_block = (inside[:, None] == inside[None, :]).astype(jnp.float32)
    q_blocks = (3.0 * diagonal[:, :, None, None] * eye_block[None, None] - product).astype(jnp.bfloat16)
    second = pattern_product(z_blocks, q_blocks, pattern)
    return (0.5 * second).astype(jnp.bfloat16)
```

```python
import functools

import jax
import jax.numpy as jnp
from jax import lax
from jax.experimental import pallas as pl
from jax.experimental.pallas import tpu as pltpu
from jax.sharding import PartitionSpec as P

HALO = 6
REACH = 2 * HALO + 1
FOLD = 16
SPLIT = ("row", "col")


def halo_rows(rows):
    count = lax.axis_size("cuts")
    return jnp.concatenate(
        [
            lax.ppermute(rows[-HALO:], "cuts", [(i, (i + 1) % count) for i in range(count)]),
            rows,
            lax.ppermute(rows[:HALO], "cuts", [((i + 1) % count, i) for i in range(count)]),
        ],
        axis=0,
    )


def product_kernel(first, left_ref, right_ref, keep_ref, *rest):
    out_ref = rest[-1]
    i = pl.program_id(0)
    depth = left_ref.shape[2]
    block = depth // REACH
    right = right_ref[pl.ds(pl.multiple_of(i * block, block), depth), :]
    total = jnp.dot(left_ref[0], right, preferred_element_type=jnp.float32)
    kept = jnp.where(keep_ref[0] > 0, total, 0.0)
    half = kept.shape[1] // 2
    folded = kept[:, :half] + kept[:, half:]
    if first:
        diagonal_ref, eye_ref = rest[:2]
        folded = diagonal_ref[0] * eye_ref[...] - folded
    else:
        folded = 0.5 * folded
    out_ref[0] = folded.astype(out_ref.dtype)


def banded_product(left, right, keep, *diagonal):
    rows, block, depth = left.shape
    lanes = right.shape[1]
    specs = [
        pl.BlockSpec((1, block, depth), lambda i: (i, 0, 0)),
        pl.BlockSpec(right.shape, lambda i: (0, 0)),
        pl.BlockSpec((1, 1, lanes), lambda i: (i, 0, 0)),
    ]
    if diagonal:
        specs.append(pl.BlockSpec((1, 1, lanes // 2), lambda i: (i, 0, 0)))
        specs.append(pl.BlockSpec((block, lanes // 2), lambda i: (0, 0)))
    return pl.pallas_call(
        functools.partial(product_kernel, bool(diagonal)),
        grid=(rows,),
        in_specs=specs,
        out_specs=pl.BlockSpec((1, block, lanes // 2), lambda i: (i, 0, 0)),
        out_shape=jax.ShapeDtypeStruct((rows, block, lanes // 2), jnp.bfloat16),
        cost_estimate=pl.CostEstimate(
            flops=2 * rows * block * depth * lanes,
            bytes_accessed=2 * (left.size + right.size),
            transcendentals=0,
        ),
    )(left, right, keep, *diagonal)


def local(y_blocks, z_blocks, pattern):
    rows, slots, part, block = y_blocks.shape
    parts = block // part
    total_rows = pattern.shape[0]
    first_row = lax.axis_index("cuts") * rows
    me = lax.axis_index("row") * lax.axis_size("col") + lax.axis_index("col")
    own = lax.dynamic_slice_in_dim(pattern, first_row, rows, 0)
    row_numbers = first_row + jnp.arange(rows, dtype=jnp.int32)
    distance = (own - row_numbers[:, None] + HALO) % total_rows
    picks = (distance[:, :, None] == jnp.arange(REACH)[None, None, :]).astype(jnp.bfloat16)

    def dense(blocks):
        spread = jnp.einsum("imd,imab->diab", picks, blocks, preferred_element_type=jnp.float32)
        spread = spread.astype(jnp.bfloat16).transpose(1, 2, 0, 3)
        return spread.reshape(rows, part, REACH * block)

    z_left = lax.all_gather(dense(z_blocks), SPLIT, axis=1, tiled=True)
    y_left = lax.all_gather(dense(y_blocks), SPLIT, axis=1, tiled=True)

    lane = jnp.arange(FOLD * part, dtype=jnp.int32)
    lane_col, lane_in = lane // part, lane % part
    depth = jnp.arange(REACH * block, dtype=jnp.int32)
    depth_col = (row_numbers[:, None] + depth[None, :] // block - HALO) % FOLD
    chooser = (
        (depth_col[:, :, None] == lane_col[None, None, :])
        & ((depth % block)[None, :, None] == (me * part + lane_in)[None, None, :])
    ).astype(jnp.bfloat16)
    z_part = jnp.einsum(
        "iak,ikl->ial", z_left, chooser, preferred_element_type=jnp.float32
    ).astype(jnp.bfloat16)

    window = first_row - HALO + jnp.arange(rows + 2 * HALO, dtype=jnp.int32)
    start = window - HALO
    column = start[:, None] + (lane_col[None, :] - start[:, None]) % FOLD
    upper = (column // FOLD) % 2
    halves = jnp.concatenate([upper == 0, upper == 1], axis=1)

    def unfolded(folded):
        folded = halo_rows(folded)
        both = jnp.concatenate([folded, folded], axis=2)
        both = jnp.where(halves[:, None, :], both, jnp.zeros_like(both))
        return both.reshape((rows + 2 * HALO) * block, 2 * FOLD * part)

    wide_col = jnp.arange(2 * FOLD * part, dtype=jnp.int32) // part
    keep = jnp.any((own % (2 * FOLD))[:, :, None] == wide_col[None, None, :], axis=1)
    keep = keep.astype(jnp.float32)[:, None, :]
    diagonal = 3.0 * (row_numbers[:, None] % FOLD == lane_col[None, :]).astype(jnp.float32)
    inside = jnp.arange(block, dtype=jnp.int32)
    eye = (inside[:, None] == (me * part + lane_in)[None, :]).astype(jnp.float32)

    q_part = banded_product(y_left, unfolded(z_part), keep, diagonal[:, None, :], eye)
    next_part = banded_product(z_left, unfolded(q_part), keep)

    sent = next_part.reshape(rows, parts, part, FOLD * part).transpose(1, 0, 2, 3)
    got = lax.all_to_all(sent, SPLIT, 0, 0, tiled=True)
    got = got.reshape(parts, rows * part, FOLD * part)
    far = jnp.arange(FOLD * block, dtype=jnp.int32)
    mover = (
        (jnp.arange(parts)[:, None, None] == ((far % block) // part)[None, None, :])
        & (lane_col[None, :, None] == (far // block)[None, None, :])
        & (lane_in[None, :, None] == (far % part)[None, None, :])
    ).astype(jnp.bfloat16)
    moved = jnp.einsum("pml,pln->mn", got, mover, preferred_element_type=jnp.float32)
    moved = moved.astype(jnp.bfloat16).reshape(rows, part, FOLD, block)
    slot_pick = ((own % FOLD)[:, :, None] == jnp.arange(FOLD)[None, None, :]).astype(jnp.bfloat16)
    out = jnp.einsum("iqc,iace->iqae", slot_pick, moved, preferred_element_type=jnp.float32)
    return out.astype(jnp.bfloat16)


def solution(mesh):
    spec = P("cuts", None, SPLIT, None)
    return jax.shard_map(
        local, mesh=mesh, in_specs=(spec, spec, P()), out_specs=spec, check_vma=False
    )
```

```python
import functools

import jax
import jax.numpy as jnp
from jax import lax
from jax.experimental import pallas as pl
from jax.experimental.pallas import tpu as pltpu
from jax.sharding import PartitionSpec as P

HALO = 6
REACH = 2 * HALO + 1
FOLD = 16
SPLIT = ("row", "col")

MESH = pl.DeviceIdType.MESH


def gather_kernel(z_ref, y_ref, z_out, y_out, send, recv, pair_send, pair_recv, own):
    core, chip, chips = lax.axis_index("row"), lax.axis_index("col"), lax.axis_size("col")
    part = z_ref.shape[1]
    other = 1 - core
    ahead, behind = lax.rem(chip + 1, chips), lax.rem(chip + chips - 1, chips)
    targets = (ahead, behind)
    ins, outs = (z_ref, y_ref), (z_out, y_out)

    barrier = pltpu.get_barrier_semaphore()
    pl.semaphore_signal(barrier, inc=1, device_id={"col": ahead}, device_id_type=MESH)
    pl.semaphore_signal(barrier, inc=1, device_id={"col": behind}, device_id_type=MESH)
    pl.semaphore_signal(barrier, inc=1, device_id={"row": other}, device_id_type=MESH)
    pl.semaphore_wait(barrier, 3)

    def place(which, at):
        at = lax.rem(at + 2 * chips, chips)
        first = pl.multiple_of((core * chips + at) * part, part)
        return outs[which].at[:, pl.ds(first, part), :]

    def pass_on(which, way, step):
        at = chip - step if way == 0 else chip + step
        there = place(which, at)
        return pltpu.make_async_remote_copy(
            src_ref=ins[which] if step == 0 else there,
            dst_ref=there,
            send_sem=send.at[which, way, step],
            recv_sem=recv.at[which, way, step],
            device_id={"col": targets[way]},
            device_id_type=MESH,
        )

    def share(which, slot, source, at):
        return pltpu.make_async_remote_copy(
            src_ref=source,
            dst_ref=place(which, at),
            send_sem=pair_send.at[which, slot],
            recv_sem=pair_recv.at[which, slot],
            device_id={"row": other},
            device_id_type=MESH,
        )

    steps = lambda which, way: chips // 2 - (1 if which != way else 0)
    arms = [(which, way) for which in range(2) for way in range(2)]
    started, waiting, kept = {}, [], []
    for which, way in arms:
        started[which, way] = pass_on(which, way, 0)
        started[which, way].start()
        waiting.append(started[which, way])
    for which in range(2):
        shared = share(which, 0, ins[which], chip)
        shared.start()
        kept.append(shared)
        mine = pltpu.make_async_copy(ins[which], place(which, chip), own.at[which])
        mine.start()
        kept.append(mine)
    for step in range(1, chips // 2 + 1):
        for which, way in arms:
            if step > steps(which, way):
                continue
            started[which, way].wait_recv()
            if step < steps(which, way):
                started[which, way] = pass_on(which, way, step)
                started[which, way].start()
                waiting.append(started[which, way])
            at = chip - step if way == 0 else chip + step
            slot = step if way == 0 else chips // 2 + step
            shared = share(which, slot, place(which, at), at)
            shared.start()
            kept.append(shared)
    for copy in waiting:
        copy.wait_send()
    for copy in kept:
        copy.wait()


def gathered(z_mine, y_mine, parts):
    rows, part, depth = z_mine.shape
    whole = jax.ShapeDtypeStruct((rows, parts * part, depth), z_mine.dtype)
    half = lax.axis_size("col") // 2
    return pl.pallas_call(
        gather_kernel,
        out_shape=(whole, whole),
        in_specs=[pl.BlockSpec(memory_space=pltpu.VMEM)] * 2,
        out_specs=(pl.BlockSpec(memory_space=pl.ANY), pl.BlockSpec(memory_space=pl.ANY)),
        scratch_shapes=[
            pltpu.SemaphoreType.DMA((2, 2, half)),
            pltpu.SemaphoreType.DMA((2, 2, half)),
            pltpu.SemaphoreType.DMA((2, 2 * half + 1)),
            pltpu.SemaphoreType.DMA((2, 2 * half + 1)),
            pltpu.SemaphoreType.DMA((2,)),
        ],
        compiler_params=pltpu.CompilerParams(collective_id=0, has_side_effects=True),
    )(z_mine, y_mine)


def halo_rows(rows):
    count = lax.axis_size("cuts")
    return jnp.concatenate(
        [
            lax.ppermute(rows[-HALO:], "cuts", [(i, (i + 1) % count) for i in range(count)]),
            rows,
            lax.ppermute(rows[:HALO], "cuts", [((i + 1) % count, i) for i in range(count)]),
        ],
        axis=0,
    )


def product_kernel(first, left_ref, right_ref, keep_ref, *rest):
    out_ref = rest[-1]
    i = pl.program_id(0)
    depth = left_ref.shape[2]
    block = depth // REACH
    right = right_ref[pl.ds(pl.multiple_of(i * block, block), depth), :]
    total = jnp.dot(left_ref[0], right, preferred_element_type=jnp.float32)
    kept = jnp.where(keep_ref[0] > 0, total, 0.0)
    half = kept.shape[1] // 2
    folded = kept[:, :half] + kept[:, half:]
    if first:
        diagonal_ref, eye_ref = rest[:2]
        folded = diagonal_ref[0] * eye_ref[...] - folded
    else:
        folded = 0.5 * folded
    out_ref[0] = folded.astype(out_ref.dtype)


def banded_product(left, right, keep, *diagonal):
    rows, block, depth = left.shape
    lanes = right.shape[1]
    specs = [
        pl.BlockSpec((1, block, depth), lambda i: (i, 0, 0)),
        pl.BlockSpec(right.shape, lambda i: (0, 0)),
        pl.BlockSpec((1, 1, lanes), lambda i: (i, 0, 0)),
    ]
    if diagonal:
        specs.append(pl.BlockSpec((1, 1, lanes // 2), lambda i: (i, 0, 0)))
        specs.append(pl.BlockSpec((block, lanes // 2), lambda i: (0, 0)))
    return pl.pallas_call(
        functools.partial(product_kernel, bool(diagonal)),
        grid=(rows,),
        in_specs=specs,
        out_specs=pl.BlockSpec((1, block, lanes // 2), lambda i: (i, 0, 0)),
        out_shape=jax.ShapeDtypeStruct((rows, block, lanes // 2), jnp.bfloat16),
        cost_estimate=pl.CostEstimate(
            flops=2 * rows * block * depth * lanes,
            bytes_accessed=2 * (left.size + right.size),
            transcendentals=0,
        ),
    )(left, right, keep, *diagonal)


def local(y_blocks, z_blocks, pattern):
    rows, slots, part, block = y_blocks.shape
    parts = block // part
    total_rows = pattern.shape[0]
    first_row = lax.axis_index("cuts") * rows
    me = lax.axis_index("row") * lax.axis_size("col") + lax.axis_index("col")
    own = lax.dynamic_slice_in_dim(pattern, first_row, rows, 0)
    row_numbers = first_row + jnp.arange(rows, dtype=jnp.int32)
    distance = (own - row_numbers[:, None] + HALO) % total_rows
    picks = (distance[:, :, None] == jnp.arange(REACH)[None, None, :]).astype(jnp.bfloat16)

    def dense(blocks):
        spread = jnp.einsum("imd,imab->diab", picks, blocks, preferred_element_type=jnp.float32)
        spread = spread.astype(jnp.bfloat16).transpose(1, 2, 0, 3)
        return spread.reshape(rows, part, REACH * block)

    z_left, y_left = gathered(dense(z_blocks), dense(y_blocks), parts)

    lane = jnp.arange(FOLD * part, dtype=jnp.int32)
    lane_col, lane_in = lane // part, lane % part
    depth = jnp.arange(REACH * block, dtype=jnp.int32)
    depth_col = (row_numbers[:, None] + depth[None, :] // block - HALO) % FOLD
    chooser = (
        (depth_col[:, :, None] == lane_col[None, None, :])
        & ((depth % block)[None, :, None] == (me * part + lane_in)[None, None, :])
    ).astype(jnp.bfloat16)
    z_part = jnp.einsum(
        "iak,ikl->ial", z_left, chooser, preferred_element_type=jnp.float32
    ).astype(jnp.bfloat16)

    window = first_row - HALO + jnp.arange(rows + 2 * HALO, dtype=jnp.int32)
    start = window - HALO
    column = start[:, None] + (lane_col[None, :] - start[:, None]) % FOLD
    upper = (column // FOLD) % 2
    halves = jnp.concatenate([upper == 0, upper == 1], axis=1)

    def unfolded(folded):
        folded = halo_rows(folded)
        both = jnp.concatenate([folded, folded], axis=2)
        both = jnp.where(halves[:, None, :], both, jnp.zeros_like(both))
        return both.reshape((rows + 2 * HALO) * block, 2 * FOLD * part)

    wide_col = jnp.arange(2 * FOLD * part, dtype=jnp.int32) // part
    keep = jnp.any((own % (2 * FOLD))[:, :, None] == wide_col[None, None, :], axis=1)
    keep = keep.astype(jnp.float32)[:, None, :]
    diagonal = 3.0 * (row_numbers[:, None] % FOLD == lane_col[None, :]).astype(jnp.float32)
    inside = jnp.arange(block, dtype=jnp.int32)
    eye = (inside[:, None] == (me * part + lane_in)[None, :]).astype(jnp.float32)

    q_part = banded_product(y_left, unfolded(z_part), keep, diagonal[:, None, :], eye)
    next_part = banded_product(z_left, unfolded(q_part), keep)

    sent = next_part.reshape(rows, parts, part, FOLD * part).transpose(1, 0, 2, 3)
    got = lax.all_to_all(sent, SPLIT, 0, 0, tiled=True)
    got = got.reshape(parts, rows * part, FOLD * part)
    far = jnp.arange(FOLD * block, dtype=jnp.int32)
    mover = (
        (jnp.arange(parts)[:, None, None] == ((far % block) // part)[None, None, :])
        & (lane_col[None, :, None] == (far // block)[None, None, :])
        & (lane_in[None, :, None] == (far % part)[None, None, :])
    ).astype(jnp.bfloat16)
    moved = jnp.einsum("pml,pln->mn", got, mover, preferred_element_type=jnp.float32)
    moved = moved.astype(jnp.bfloat16).reshape(rows, part, FOLD, block)
    slot_pick = ((own % FOLD)[:, :, None] == jnp.arange(FOLD)[None, None, :]).astype(jnp.bfloat16)
    out = jnp.einsum("iqc,iace->iqae", slot_pick, moved, preferred_element_type=jnp.float32)
    return out.astype(jnp.bfloat16)


def solution(mesh):
    spec = P("cuts", None, SPLIT, None)
    return jax.shard_map(
        local, mesh=mesh, in_specs=(spec, spec, P()), out_specs=spec, check_vma=False
    )
```
